32 devices in a mesh: depth: 2 (over y), vx: 4 (over x, core), vy: 4 (over z).
Axes of the slice: x: 2, y: 2, z: 4, core: 2. Of those that a mesh axis runs over, the one named last changes fastest.
Arguments:
- token_ids: int32 [130], replicated, may hold values from 0 to 8191
- hidden: bfloat16 [2, 128, 7168], P('depth', ('vx', 'vy')), may hold values from -50 to 50
- gain: float32 [2, 7168], P('depth'), may hold values from 0.5 to 1.5
- embedding: bfloat16 [8192, 7168], P('vx', 'vy'), may hold values from -0.6 to 0.6
Outputs:
- row_loss: float32 [128], P(('vx', 'vy'))
The draws below stay inside these ranges and needn't reach their ends.
All inputs are finite; a program needn't handle non-finite values.
Results may differ from the reference program's by a relative error of at most 0.00044.
Values may be sent and summed in bfloat16 or wider, within the bound.
A program may use at most 128 MiB of HBM per device.

```python
import math
import jax
import jax.numpy as jnp
from jax import lax

D = 7168
HEADS = 2
VOCAB = 8192
ROWS = 128


def drawn(key):
    signs = 2.0 * jax.random.randint(jax.random.fold_in(key, 21), (4, D), 0, 2).astype(jnp.float32) - 1.0
    chosen = jax.random.permutation(jax.random.fold_in(key, 22), VOCAB)[:8]
    gaps = jax.random.randint(jax.random.fold_in(key, 23), (4,), 1, 4).astype(jnp.float32)
    return (signs, chosen, gaps)


def draw_embedding(key, part):
    values = jax.random.normal(jax.random.fold_in(key, 11), (VOCAB, D), jnp.float32)
    table = 0.05 * jnp.clip(values, -6.0, 6.0)
    signs, chosen, gaps = drawn(key)
    levels = jnp.array([100.0, 110.0, 120.0, 130.0], jnp.float32)
    upper = signs * (levels / D)[:, None]
    lower = signs * ((levels - gaps) / D)[:, None]
    rows = jnp.stack([upper, lower], axis=1).reshape(8, D)
    table = table.at[chosen].set(rows)
    return table.astype(jnp.bfloat16)


def draw_hidden(key, part):
    base = jnp.clip(jax.random.normal(jax.random.fold_in(key, 12), (HEADS, ROWS, D), jnp.float32), -6.0, 6.0)
    signs, chosen, gaps = drawn(key)
    factors = jax.random.uniform(jax.random.fold_in(key, 24), (HEADS, 4, 1), jnp.float32, 1.0, 20.0)
    aligned = factors * signs[None, :, :]
    picks = jnp.stack([jax.random.permutation(jax.random.fold_in(key, 30 + head), ROWS)[:4] for head in range(HEADS)])
    heads_index = jnp.arange(HEADS)[:, None]
    base = base.at[heads_index, picks].set(aligned)
    return base.astype(jnp.bfloat16)


def touch_ends(entries, key, smallest, top_value):
    extent = entries.shape
    index_at = [jax.random.randint(jax.random.fold_in(key, axis), (), 0, extent[axis]) for axis in range(len(extent))]
    entries = entries.at[tuple(index_at)].set(smallest)
    longest = extent.index(max(extent))
    index_at[longest] = (index_at[longest] + 1) % extent[longest]
    return entries.at[tuple(index_at)].set(top_value)


def setup_inputs(seed: int = 0) -> dict:
    arg_keys = jax.random.split(jax.random.key(seed), 5)
    return {
        "token_ids": touch_ends(jax.random.randint(arg_keys[0], (ROWS + HEADS,), 0, VOCAB), jax.random.fold_in(arg_keys[0], 1), 0, VOCAB - 1).astype(jnp.int32),
        "hidden": draw_hidden(jax.random.fold_in(arg_keys[4], 71), 0),
        "gain": jnp.clip(1.0 + 0.1 * jax.random.normal(arg_keys[2], (HEADS, D), jnp.float32), 0.5, 1.5),
        "embedding": draw_embedding(jax.random.fold_in(arg_keys[4], 71), 0),
    }


EPS = 1e-06

def head_loss(rows, gain_row, embedding, targets):
    values = rows.astype(jnp.float32)
    scale = lax.rsqrt(lax.optimization_barrier(jnp.mean(values * values, axis=1, keepdims=True)) + EPS)
    normed = (values * scale * gain_row[None, :]).astype(jnp.bfloat16)
    block = math.gcd(ROWS, 512)

    def one(pair):
        piece, wanted = pair
        logits = lax.dot_general(piece, embedding, (((1,), (1,)), ((), ())), preferred_element_type=jnp.float32)
        peak = lax.optimization_barrier(jnp.max(logits, axis=1))
        total = lax.optimization_barrier(jnp.sum(jnp.exp(logits - peak[:, None]), axis=1))
        picked = jnp.take_along_axis(logits, wanted[:, None], axis=1)[:, 0]
        return peak + jnp.log(total) - picked
    losses = lax.map(one, (normed.reshape(-1, block, D), targets.reshape(-1, block)))
    return losses.reshape(-1)

def reference(token_ids, hidden, gain, embedding):
    summed = jnp.zeros((ROWS,), jnp.float32)
    for head in range(HEADS):
        targets = token_ids[head + 1:head + 1 + ROWS]
        summed = summed + head_loss(hidden[head], gain[head], embedding, targets)
    return summed
```

```python
import functools

import jax
import jax.numpy as jnp
from jax import lax
from jax.experimental import pallas as pl
from jax.experimental.pallas import tpu as pltpu
from jax.sharding import PartitionSpec as P

EPS = 1e-06
MESH = pl.DeviceIdType.MESH
LANES = 128
TILE = 256
LAG = 2
NT = (((1,), (1,)), ((), ()))


def kernel(
    sizes, tok_ref, hid_ref, gain_ref, emb_hbm, out_ref,
    emb, nx, xg, xall, acc, send_buf, recv_buf, fin, st, rx,
    esem, sa, ra, sb, rb, cs, cr, ss, rs,
):
    heads, nvx, nvy = sizes
    d, i, j = lax.axis_index("depth"), lax.axis_index("vx"), lax.axis_index("vy")
    rows_dev = nx.shape[1]
    cols = nx.shape[2]
    half = emb.shape[0] // 2
    tiles = half // TILE
    pairs = nvx // 2
    pieces = pairs * tiles
    pair_rows = xall.shape[1]

    parts = esem.shape[0]
    block = emb.shape[0] // parts
    loads = [
        pltpu.make_async_copy(
            emb_hbm.at[pl.ds(k * block, block)], emb.at[pl.ds(k * block, block)], esem.at[k]
        )
        for k in range(parts)
    ]
    for load in loads:
        load.start()

    barrier = pltpu.get_barrier_semaphore()
    for k in range(1, nvy):
        pl.semaphore_signal(barrier, inc=1, device_id=(d, i, lax.rem(j + k, nvy)), device_id_type=MESH)
    for k in range(1, nvx):
        pl.semaphore_signal(barrier, inc=1, device_id=(d, lax.rem(i + k, nvx), j), device_id_type=MESH)
    for k in range(1, heads):
        pl.semaphore_signal(barrier, inc=1, device_id=(lax.rem(d + k, heads), i, j), device_id_type=MESH)

    values = hid_ref[0].astype(jnp.float32)
    scale = lax.rsqrt(jnp.mean(values * values, axis=1, keepdims=True) + EPS)
    normed = (values * scale * gain_ref[...]).astype(jnp.bfloat16)
    for k in range(nvy):
        nx[k] = normed[:, k * cols:(k + 1) * cols]
    xg[i, j] = nx[j]
    pl.semaphore_wait(barrier, nvy - 1 + nvx - 1 + heads - 1)

    first = []
    for k in range(1, nvy):
        to = lax.rem(j + k, nvy)
        copy = pltpu.make_async_remote_copy(
            src_ref=nx.at[to], dst_ref=xg.at[i, j], send_sem=sa.at[to], recv_sem=ra.at[j],
            device_id=(d, i, to), device_id_type=MESH,
        )
        copy.start()
        first.append(copy)

    second = []
    for k in range(nvy):
        src = lax.rem(j + k, nvy)
        if k:
            pltpu.make_async_remote_copy(
                src_ref=nx.at[src], dst_ref=xg.at[i, src], send_sem=sa.at[src], recv_sem=ra.at[src],
                device_id=(d, i, src), device_id_type=MESH,
            ).wait_recv()
        for m in range(1, nvx):
            to = lax.rem(i + m, nvx)
            copy = pltpu.make_async_remote_copy(
                src_ref=xg.at[i, src], dst_ref=xg.at[i, src],
                send_sem=sb.at[to, src], recv_sem=rb.at[i, src],
                device_id=(d, to, j), device_id_type=MESH,
            )
            copy.start()
            second.append(copy)

    def ready(p):
        q = lax.rem(i // 2 + p, pairs)

        def arrived(c):
            b = 2 * q + c

            @pl.when(b != i)
            def _():
                for src in range(nvy):
                    pltpu.make_async_remote_copy(
                        src_ref=xg.at[b, src], dst_ref=xg.at[b, src],
                        send_sem=sb.at[b, src], recv_sem=rb.at[b, src],
                        device_id=(d, b, j), device_id_type=MESH,
                    ).wait_recv()

        arrived(0)
        arrived(1)
        both = xg[pl.ds(2 * q, 2)].astype(jnp.float32)
        xall[q] = both.reshape(pair_rows, cols).astype(jnp.bfloat16)

    for load in loads:
        load.wait()

    def hop(way, k, to):
        return pltpu.make_async_remote_copy(
            src_ref=send_buf.at[way, k], dst_ref=recv_buf.at[way, k],
            send_sem=cs.at[way, k], recv_sem=cr.at[way, k],
            device_id=(d, i, to), device_id_type=MESH,
        )

    def advance(way, k, place, to):
        q = lax.rem(i // 2 + k // tiles, pairs)
        t = lax.rem(k, tiles)
        start = pl.multiple_of((1 - way) * half + t * TILE, TILE)
        acc[...] = lax.dot_general(
            xall[q], emb[pl.ds(start, TILE), :], NT, preferred_element_type=jnp.float32
        )

        @pl.when(place > 0)
        def _():
            hop(way, k, to).wait_recv()
            acc[...] += recv_buf[way, k]

        @pl.when(place < nvy - 1)
        def _():
            send_buf[way, k] = acc[...]
            hop(way, k, to).start()

        @pl.when(place == nvy - 1)
        def _():
            fin[q, t] = acc[...]

    up, down = j, nvy - 1 - j
    above, below = jnp.minimum(j + 1, nvy - 1), jnp.maximum(j - 1, 0)
    near = jnp.minimum(up, down)

    def step(s, carry):
        k0 = s - LAG * up
        k1 = s - LAG * down
        p = (s - LAG * near) // tiles

        @pl.when((s >= LAG * near) & (s < LAG * near + pieces) & (lax.rem(s - LAG * near, tiles) == 0))
        def _():
            ready(p)

        @pl.when((k0 >= 0) & (k0 < pieces))
        def _():
            advance(0, k0, up, above)

        @pl.when((k1 >= 0) & (k1 < pieces))
        def _():
            advance(1, k1, down, below)

        return carry

    lax.fori_loop(0, pieces + LAG * (nvy - 1), step, 0)

    at_end = (j == 0) | (j == nvy - 1)
    end = jnp.where(j == 0, 0, 1)
    slot = (d * 2 + end) * nvx + i
    owners = pair_rows // rows_dev

    def stat_copy(head, owner_x, owner_y):
        owner = owner_x * nvy + owner_y
        return pltpu.make_async_remote_copy(
            src_ref=st.at[owner], dst_ref=rx.at[slot],
            send_sem=ss.at[head * nvx * nvy + owner], recv_sem=rs.at[slot],
            device_id=(head, owner_x, owner_y), device_id_type=MESH,
        )

    @pl.when(at_end)
    def _():
        base = (i * 2 + jnp.where(j == 0, 0, 1)) * half
        tok = tok_ref[...].astype(jnp.float32)
        for q in range(pairs):
            logits = fin[q]
            peak = jnp.max(jnp.max(logits, axis=0), axis=1, keepdims=True)
            total = jnp.sum(jnp.sum(jnp.exp(logits - peak[None]), axis=0), axis=1, keepdims=True)
            at = lax.broadcasted_iota(jnp.int32, (pair_rows, tok.shape[1]), 1)
            row = lax.broadcasted_iota(jnp.int32, (pair_rows, tok.shape[1]), 0)
            wanted = jnp.sum(
                jnp.where(at == row + (q * pair_rows + d + 1), tok, 0.0), axis=1, keepdims=True
            )
            column = lax.broadcasted_iota(jnp.int32, (pair_rows, TILE), 1)
            hit = jnp.zeros((pair_rows, TILE), jnp.float32)
            for t in range(tiles):
                here = (column + (base + t * TILE)).astype(jnp.float32)
                hit = hit + jnp.where(here == wanted, logits[t], 0.0)
            picked = jnp.sum(hit, axis=1, keepdims=True)
            lane = lax.broadcasted_iota(jnp.int32, (pair_rows, LANES), 1)
            sub = lax.rem(lax.broadcasted_iota(jnp.int32, (pair_rows, LANES), 0), rows_dev)
            packed = jnp.where(lane == sub, peak, 0.0)
            packed = packed + jnp.where(lane == sub + rows_dev, total, 0.0)
            packed = packed + jnp.where(lane == sub + 2 * rows_dev, picked, 0.0)
            packed = jnp.sum(packed.reshape(owners, rows_dev, LANES), axis=1)
            for o in range(owners):
                st[q * owners + o] = packed[o:o + 1]
        rx[slot] = st[i * nvy + j]
        for head in range(heads):
            for x in range(nvx):
                for y in range(nvy):
                    @pl.when((head != d) | (x != i) | (y != j))
                    def _(head=head, x=x, y=y):
                        stat_copy(head, x, y).start()

    for s in range(heads * 2 * nvx):
        head, rest = divmod(s, 2 * nvx)
        side, x = divmod(rest, nvx)
        y = side * (nvy - 1)

        @pl.when((head != d) | (x != i) | (y != j))
        def _(s=s, head=head, x=x, y=y):
            pltpu.make_async_remote_copy(
                src_ref=st.at[0], dst_ref=rx.at[s], send_sem=ss.at[0], recv_sem=rs.at[s],
                device_id=(head, x, y), device_id_type=MESH,
            ).wait_recv()

    result = jnp.zeros((1, LANES), jnp.float32)
    for head in range(heads):
        block = rx[pl.ds(head * 2 * nvx, 2 * nvx)]
        sums = pltpu.roll(block, LANES - rows_dev, 2)
        picks = pltpu.roll(block, LANES - 2 * rows_dev, 2)
        peak = jnp.max(block, axis=0)
        total = jnp.sum(sums * jnp.exp(block - peak[None]), axis=0)
        result = result + (peak + jnp.log(total) - jnp.sum(picks, axis=0))
    out_ref[...] = result[:, :rows_dev]

    for copy in first + second:
        copy.wait_send()

    def drain(k, carry):
        @pl.when(up < nvy - 1)
        def _():
            hop(0, k, above).wait_send()

        @pl.when(down < nvy - 1)
        def _():
            hop(1, k, below).wait_send()

        return carry

    lax.fori_loop(0, pieces, drain, 0)

    @pl.when(at_end)
    def _():
        for head in range(heads):
            for x in range(nvx):
                for y in range(nvy):
                    @pl.when((head != d) | (x != i) | (y != j))
                    def _(head=head, x=x, y=y):
                        stat_copy(head, x, y).wait_send()


def body(sizes, token_ids, hidden, gain, embedding):
    heads, nvx, nvy = sizes
    rows_dev, width = hidden.shape[1:]
    cols = width // nvy
    pairs = nvx // 2
    pair_rows = 2 * nvy * rows_dev
    tiles = embedding.shape[0] // 2 // TILE
    pieces = pairs * tiles
    dma = pltpu.SemaphoreType.DMA
    vmem = pl.BlockSpec(memory_space=pltpu.VMEM)
    out = pl.pallas_call(
        functools.partial(kernel, sizes),
        out_shape=jax.ShapeDtypeStruct((1, rows_dev), jnp.float32),
        in_specs=[vmem, vmem, vmem, pl.BlockSpec(memory_space=pl.ANY)],
        out_specs=vmem,
        scratch_shapes=[
            pltpu.VMEM(embedding.shape, embedding.dtype),
            pltpu.VMEM((nvy, rows_dev, cols), jnp.bfloat16),
            pltpu.VMEM((nvx, nvy, rows_dev, cols), jnp.bfloat16),
            pltpu.VMEM((pairs, pair_rows, cols), jnp.bfloat16),
            pltpu.VMEM((pair_rows, TILE), jnp.float32),
            pltpu.VMEM((2, pieces, pair_rows, TILE), jnp.float32),
            pltpu.VMEM((2, pieces, pair_rows, TILE), jnp.float32),
            pltpu.VMEM((pairs, tiles, pair_rows, TILE), jnp.float32),
            pltpu.VMEM((nvx * nvy, 1, LANES), jnp.float32),
            pltpu.VMEM((heads * 2 * nvx, 1, LANES), jnp.float32),
            dma((4,)),
            dma((nvy,)),
            dma((nvy,)),
            dma((nvx, nvy)),
            dma((nvx, nvy)),
            dma((2, pieces)),
            dma((2, pieces)),
            dma((heads * nvx * nvy,)),
            dma((heads * 2 * nvx,)),
        ],
        compiler_params=pltpu.CompilerParams(
            collective_id=0, has_side_effects=True, vmem_limit_bytes=62 * 1024 * 1024
        ),
    )(token_ids.reshape(1, -1), hidden, gain, embedding)
    return out.reshape(rows_dev)


def solution(mesh):
    sizes = (mesh.shape["depth"], mesh.shape["vx"], mesh.shape["vy"])
    in_specs = (P(), P("depth", ("vx", "vy"), None), P("depth", None), P("vx", "vy"))
    out_specs = P(("vx", "vy"))
    return jax.shard_map(
        functools.partial(body, sizes), mesh=mesh, in_specs=in_specs, out_specs=out_specs, check_vma=False
    )
```

```python
import functools

import jax
import jax.numpy as jnp
from jax import lax
from jax.experimental import pallas as pl
from jax.experimental.pallas import tpu as pltpu
from jax.sharding import PartitionSpec as P

EPS = 1e-06
MESH = pl.DeviceIdType.MESH
LANES = 128
TILE = 512
LAG = 2
TOP = 32767.0
TINY = 1e-30
NT = (((1,), (1,)), ((), ()))


def kernel(
    sizes, tok_ref, hid_ref, gain_ref, emb_hbm, out_ref,
    emb, nx, xg, xall, acc, send_buf, recv_buf, fin, st, rx,
    gauge_out, gauge_in, esem, sa, ra, sb, rb, cs, cr, gs, gr, ss, rs,
):
    heads, nvx, nvy = sizes
    d, i, j = lax.axis_index("depth"), lax.axis_index("vx"), lax.axis_index("vy")
    rows_dev = nx.shape[1]
    cols = nx.shape[2]
    half = emb.shape[0] // 2
    tiles = half // TILE
    pairs = nvx // 2
    pieces = pairs * tiles
    pair_rows = xall.shape[1]

    parts = esem.shape[0]
    block = emb.shape[0] // parts
    loads = [
        pltpu.make_async_copy(
            emb_hbm.at[pl.ds(k * block, block)], emb.at[pl.ds(k * block, block)], esem.at[k]
        )
        for k in range(parts)
    ]
    for load in loads:
        load.start()

    barrier = pltpu.get_barrier_semaphore()
    for k in range(1, nvy):
        pl.semaphore_signal(barrier, inc=1, device_id=(d, i, lax.rem(j + k, nvy)), device_id_type=MESH)
    for k in range(1, nvx):
        pl.semaphore_signal(barrier, inc=1, device_id=(d, lax.rem(i + k, nvx), j), device_id_type=MESH)
    for k in range(1, heads):
        pl.semaphore_signal(barrier, inc=1, device_id=(lax.rem(d + k, heads), i, j), device_id_type=MESH)

    values = hid_ref[0].astype(jnp.float32)
    scale = lax.rsqrt(jnp.mean(values * values, axis=1, keepdims=True) + EPS)
    normed = (values * scale * gain_ref[...]).astype(jnp.bfloat16)
    for k in range(nvy):
        nx[k] = normed[:, k * cols:(k + 1) * cols]
    xg[i, j] = nx[j]
    pl.semaphore_wait(barrier, nvy - 1 + nvx - 1 + heads - 1)

    first = []
    for k in range(1, nvy):
        to = lax.rem(j + k, nvy)
        copy = pltpu.make_async_remote_copy(
            src_ref=nx.at[to], dst_ref=xg.at[i, j], send_sem=sa.at[to], recv_sem=ra.at[j],
            device_id=(d, i, to), device_id_type=MESH,
        )
        copy.start()
        first.append(copy)

    second = []
    for k in range(nvy):
        src = lax.rem(j + k, nvy)
        if k:
            pltpu.make_async_remote_copy(
                src_ref=nx.at[src], dst_ref=xg.at[i, src], send_sem=sa.at[src], recv_sem=ra.at[src],
                device_id=(d, i, src), device_id_type=MESH,
            ).wait_recv()
        for m in range(1, nvx):
            to = lax.rem(i + m, nvx)
            copy = pltpu.make_async_remote_copy(
                src_ref=xg.at[i, src], dst_ref=xg.at[i, src],
                send_sem=sb.at[to, src], recv_sem=rb.at[i, src],
                device_id=(d, to, j), device_id_type=MESH,
            )
            copy.start()
            second.append(copy)

    def ready(p):
        q = lax.rem(i // 2 + p, pairs)

        def arrived(c):
            b = 2 * q + c

            @pl.when(b != i)
            def _():
                for src in range(nvy):
                    pltpu.make_async_remote_copy(
                        src_ref=xg.at[b, src], dst_ref=xg.at[b, src],
                        send_sem=sb.at[b, src], recv_sem=rb.at[b, src],
                        device_id=(d, b, j), device_id_type=MESH,
                    ).wait_recv()

        arrived(0)
        arrived(1)
        both = xg[pl.ds(2 * q, 2)].astype(jnp.float32)
        xall[q] = both.reshape(pair_rows, cols).astype(jnp.bfloat16)

    for load in loads:
        load.wait()

    def hop(way, k, to):
        return pltpu.make_async_remote_copy(
            src_ref=send_buf.at[way, k], dst_ref=recv_buf.at[way, k],
            send_sem=cs.at[way, k], recv_sem=cr.at[way, k],
            device_id=(d, i, to), device_id_type=MESH,
        )

    def gauge(way, k, to):
        return pltpu.make_async_remote_copy(
            src_ref=gauge_out.at[way, k], dst_ref=gauge_in.at[way, k],
            send_sem=gs.at[way, k], recv_sem=gr.at[way, k],
            device_id=(d, i, to), device_id_type=MESH,
        )

    def advance(way, k, place, to):
        q = lax.rem(i // 2 + k // tiles, pairs)
        t = lax.rem(k, tiles)
        start = pl.multiple_of((1 - way) * half + t * TILE, TILE)
        acc[...] = lax.dot_general(
            xall[q], emb[pl.ds(start, TILE), :], NT, preferred_element_type=jnp.float32
        )

        @pl.when(place > 0)
        def _():
            gauge(way, k, to).wait_recv()
            hop(way, k, to).wait_recv()
            acc[...] += recv_buf[way, k].astype(jnp.float32) * gauge_in[way, k]

        @pl.when(place < nvy - 1)
        def _():
            partial = acc[...]
            span = jnp.maximum(jnp.max(jnp.abs(partial), axis=0, keepdims=True), TINY)
            gauge_out[way, k] = span * (1.0 / TOP)
            send_buf[way, k] = jnp.round(partial * (TOP / span)).astype(jnp.int32).astype(jnp.int16)
            hop(way, k, to).start()
            gauge(way, k, to).start()

        @pl.when(place == nvy - 1)
        def _():
            fin[q, t] = acc[...]

    up, down = j, nvy - 1 - j
    above, below = jnp.minimum(j + 1, nvy - 1), jnp.maximum(j - 1, 0)
    near = jnp.minimum(up, down)

    def step(s, carry):
        k0 = s - LAG * up
        k1 = s - LAG * down
        p = (s - LAG * near) // tiles

        @pl.when((s >= LAG * near) & (s < LAG * near + pieces) & (lax.rem(s - LAG * near, tiles) == 0))
        def _():
            ready(p)

        @pl.when((k0 >= 0) & (k0 < pieces))
        def _():
            advance(0, k0, up, above)

        @pl.when((k1 >= 0) & (k1 < pieces))
        def _():
            advance(1, k1, down, below)

        return carry

    lax.fori_loop(0, pieces + LAG * (nvy - 1), step, 0)

    at_end = (j == 0) | (j == nvy - 1)
    end = jnp.where(j == 0, 0, 1)
    slot = (d * 2 + end) * nvx + i
    owners = pair_rows // rows_dev

    def stat_copy(head, owner_x, owner_y):
        owner = owner_x * nvy + owner_y
        return pltpu.make_async_remote_copy(
            src_ref=st.at[owner], dst_ref=rx.at[slot],
            send_sem=ss.at[head * nvx * nvy + owner], recv_sem=rs.at[slot],
            device_id=(head, owner_x, owner_y), device_id_type=MESH,
        )

    @pl.when(at_end)
    def _():
        base = (i * 2 + jnp.where(j == 0, 0, 1)) * half
        tok = tok_ref[...].astype(jnp.float32)
        for q in range(pairs):
            logits = fin[q]
            peak = jnp.max(jnp.max(logits, axis=0), axis=1, keepdims=True)
            total = jnp.sum(jnp.sum(jnp.exp(logits - peak[None]), axis=0), axis=1, keepdims=True)
            at = lax.broadcasted_iota(jnp.int32, (pair_rows, tok.shape[1]), 1)
            row = lax.broadcasted_iota(jnp.int32, (pair_rows, tok.shape[1]), 0)
            wanted = jnp.sum(
                jnp.where(at == row + (q * pair_rows + d + 1), tok, 0.0), axis=1, keepdims=True
            )
            column = lax.broadcasted_iota(jnp.int32, (pair_rows, TILE), 1)
            hit = jnp.zeros((pair_rows, TILE), jnp.float32)
            for t in range(tiles):
                here = (column + (base + t * TILE)).astype(jnp.float32)
                hit = hit + jnp.where(here == wanted, logits[t], 0.0)
            picked = jnp.sum(hit, axis=1, keepdims=True)
            lane = lax.broadcasted_iota(jnp.int32, (pair_rows, LANES), 1)
            sub = lax.rem(lax.broadcasted_iota(jnp.int32, (pair_rows, LANES), 0), rows_dev)
            packed = jnp.where(lane == sub, peak, 0.0)
            packed = packed + jnp.where(lane == sub + rows_dev, total, 0.0)
            packed = packed + jnp.where(lane == sub + 2 * rows_dev, picked, 0.0)
            packed = jnp.sum(packed.reshape(owners, rows_dev, LANES), axis=1)
            for o in range(owners):
                st[q * owners + o] = packed[o:o + 1]
        rx[slot] = st[i * nvy + j]
        for head in range(heads):
            for x in range(nvx):
                for y in range(nvy):
                    @pl.when((head != d) | (x != i) | (y != j))
                    def _(head=head, x=x, y=y):
                        stat_copy(head, x, y).start()

    for s in range(heads * 2 * nvx):
        head, rest = divmod(s, 2 * nvx)
        side, x = divmod(rest, nvx)
        y = side * (nvy - 1)

        @pl.when((head != d) | (x != i) | (y != j))
        def _(s=s, head=head, x=x, y=y):
            pltpu.make_async_remote_copy(
                src_ref=st.at[0], dst_ref=rx.at[s], send_sem=ss.at[0], recv_sem=rs.at[s],
                device_id=(head, x, y), device_id_type=MESH,
            ).wait_recv()

    result = jnp.zeros((1, LANES), jnp.float32)
    for head in range(heads):
        block = rx[pl.ds(head * 2 * nvx, 2 * nvx)]
        sums = pltpu.roll(block, LANES - rows_dev, 2)
        picks = pltpu.roll(block, LANES - 2 * rows_dev, 2)
        peak = jnp.max(block, axis=0)
        total = jnp.sum(sums * jnp.exp(block - peak[None]), axis=0)
        result = result + (peak + jnp.log(total) - jnp.sum(picks, axis=0))
    out_ref[...] = result[:, :rows_dev]

    for copy in first + second:
        copy.wait_send()

    def drain(k, carry):
        @pl.when(up < nvy - 1)
        def _():
            hop(0, k, above).wait_send()
            gauge(0, k, above).wait_send()

        @pl.when(down < nvy - 1)
        def _():
            hop(1, k, below).wait_send()
            gauge(1, k, below).wait_send()

        return carry

    lax.fori_loop(0, pieces, drain, 0)

    @pl.when(at_end)
    def _():
        for head in range(heads):
            for x in range(nvx):
                for y in range(nvy):
                    @pl.when((head != d) | (x != i) | (y != j))
                    def _(head=head, x=x, y=y):
                        stat_copy(head, x, y).wait_send()


def body(sizes, token_ids, hidden, gain, embedding):
    heads, nvx, nvy = sizes
    rows_dev, width = hidden.shape[1:]
    cols = width // nvy
    pairs = nvx // 2
    pair_rows = 2 * nvy * rows_dev
    tiles = embedding.shape[0] // 2 // TILE
    pieces = pairs * tiles
    dma = pltpu.SemaphoreType.DMA
    vmem = pl.BlockSpec(memory_space=pltpu.VMEM)
    out = pl.pallas_call(
        functools.partial(kernel, sizes),
        out_shape=jax.ShapeDtypeStruct((1, rows_dev), jnp.float32),
        in_specs=[vmem, vmem, vmem, pl.BlockSpec(memory_space=pl.ANY)],
        out_specs=vmem,
        scratch_shapes=[
            pltpu.VMEM(embedding.shape, embedding.dtype),
            pltpu.VMEM((nvy, rows_dev, cols), jnp.bfloat16),
            pltpu.VMEM((nvx, nvy, rows_dev, cols), jnp.bfloat16),
            pltpu.VMEM((pairs, pair_rows, cols), jnp.bfloat16),
            pltpu.VMEM((pair_rows, TILE), jnp.float32),
            pltpu.VMEM((2, pieces, pair_rows, TILE), jnp.int16),
            pltpu.VMEM((2, pieces, pair_rows, TILE), jnp.int16),
            pltpu.VMEM((pairs, tiles, pair_rows, TILE), jnp.float32),
            pltpu.VMEM((nvx * nvy, 1, LANES), jnp.float32),
            pltpu.VMEM((heads * 2 * nvx, 1, LANES), jnp.float32),
            pltpu.VMEM((2, pieces, 1, TILE), jnp.float32),
            pltpu.VMEM((2, pieces, 1, TILE), jnp.float32),
            dma((4,)),
            dma((nvy,)),
            dma((nvy,)),
            dma((nvx, nvy)),
            dma((nvx, nvy)),
            dma((2, pieces)),
            dma((2, pieces)),
            dma((2, pieces)),
            dma((2, pieces)),
            dma((heads * nvx * nvy,)),
            dma((heads * 2 * nvx,)),
        ],
        compiler_params=pltpu.CompilerParams(
            collective_id=0, has_side_effects=True, vmem_limit_bytes=62 * 1024 * 1024
        ),
    )(token_ids.reshape(1, -1), hidden, gain, embedding)
    return out.reshape(rows_dev)


def solution(mesh):
    sizes = (mesh.shape["depth"], mesh.shape["vx"], mesh.shape["vy"])
    in_specs = (P(), P("depth", ("vx", "vy"), None), P("depth", None), P("vx", "vy"))
    out_specs = P(("vx", "vy"))
    return jax.shard_map(
        functools.partial(body, sizes), mesh=mesh, in_specs=in_specs, out_specs=out_specs, check_vma=False
    )
```

```python
import functools

import jax
import jax.numpy as jnp
from jax import lax
from jax.experimental import pallas as pl
from jax.experimental.pallas import tpu as pltpu
from jax.sharding import PartitionSpec as P

EPS = 1e-06
MESH = pl.DeviceIdType.MESH
LANES = 128
TILE = 512
LAG = 2
TOP = 32767.0
TINY = 1e-30
NT = (((1,), (1,)), ((), ()))


def kernel(
    sizes, tok_ref, hid_ref, gain_ref, emb_hbm, out_ref,
    emb, nx, xg, xall, acc, send_buf, recv_buf, fin, st, rx,
    gauge_out, gauge_in, esem, sa, ra, sb, rb, cs, cr, gs, gr, ss, rs,
):
    heads, nvx, nvy = sizes
    d, i, j = lax.axis_index("depth"), lax.axis_index("vx"), lax.axis_index("vy")
    rows_dev = nx.shape[1]
    cols = nx.shape[2]
    half = emb.shape[0] // 2
    tiles = half // TILE
    pairs = nvx // 2
    pieces = pairs * tiles
    pair_rows = xall.shape[1]

    parts = esem.shape[0]
    block = emb.shape[0] // parts
    loads = [
        pltpu.make_async_copy(
            emb_hbm.at[pl.ds(k * block, block)], emb.at[pl.ds(k * block, block)], esem.at[k]
        )
        for k in range(parts)
    ]
    for load in loads:
        load.start()

    barrier = pltpu.get_barrier_semaphore()
    for k in range(1, nvy):
        pl.semaphore_signal(barrier, inc=1, device_id=(d, i, lax.rem(j + k, nvy)), device_id_type=MESH)
    for k in range(1, nvx):
        pl.semaphore_signal(barrier, inc=1, device_id=(d, lax.rem(i + k, nvx), j), device_id_type=MESH)
    for k in range(1, heads):
        pl.semaphore_signal(barrier, inc=1, device_id=(lax.rem(d + k, heads), i, j), device_id_type=MESH)

    values = hid_ref[0].astype(jnp.float32)
    scale = lax.rsqrt(jnp.mean(values * values, axis=1, keepdims=True) + EPS)
    normed = (values * scale * gain_ref[...]).astype(jnp.bfloat16)
    for k in range(nvy):
        nx[k] = normed[:, k * cols:(k + 1) * cols]
    xg[i, j] = nx[j]
    pl.semaphore_wait(barrier, nvy - 1 + nvx - 1 + heads - 1)

    def column_copy(to, src):
        return pltpu.make_async_remote_copy(
            src_ref=nx.at[to], dst_ref=xg.at[i, src], send_sem=sa.at[to], recv_sem=ra.at[src],
            device_id=(d, i, to), device_id_type=MESH,
        )

    for far in reversed(range(1, nvy)):
        @pl.when(j + far < nvy)
        def _(far=far):
            column_copy(j + far, j).start()

        @pl.when(j - far >= 0)
        def _(far=far):
            column_copy(j - far, j).start()

    sibling = i + 1 - 2 * lax.rem(i, 2)

    def slice_copy(b, src, to, sem):
        return pltpu.make_async_remote_copy(
            src_ref=xg.at[b, src], dst_ref=xg.at[b, src],
            send_sem=sb.at[sem, src], recv_sem=rb.at[b, src],
            device_id=(d, to, j), device_id_type=MESH,
        )

    def spread(src):
        for m in range(1, pairs):
            to = lax.rem(i + 2 * m, nvx)
            slice_copy(i, src, to, to).start()
        slice_copy(i, src, sibling, sibling).start()

    spread(j)
    for far in range(1, nvy):
        @pl.when(j + far < nvy)
        def _(far=far):
            column_copy(j + far, j + far).wait_recv()
            spread(j + far)

        @pl.when(j - far >= 0)
        def _(far=far):
            column_copy(j - far, j - far).wait_recv()
            spread(j - far)

    def ready(p):
        q = lax.rem(i // 2 + p, pairs)
        same = 2 * q + lax.rem(i, 2)
        other = 2 * q + 1 - lax.rem(i, 2)

        @pl.when(p > 0)
        def _():
            for src in range(nvy):
                slice_copy(same, src, sibling, other).wait_recv()
                slice_copy(same, src, sibling, other).start()

        for src in range(nvy):
            slice_copy(other, src, other, other).wait_recv()
        both = xg[pl.ds(2 * q, 2)].astype(jnp.float32)
        xall[q] = both.reshape(pair_rows, cols).astype(jnp.bfloat16)

    for load in loads:
        load.wait()

    def hop(way, k, to):
        return pltpu.make_async_remote_copy(
            src_ref=send_buf.at[way, k], dst_ref=recv_buf.at[way, k],
            send_sem=cs.at[way, k], recv_sem=cr.at[way, k],
            device_id=(d, i, to), device_id_type=MESH,
        )

    def gauge(way, k, to):
        return pltpu.make_async_remote_copy(
            src_ref=gauge_out.at[way, k], dst_ref=gauge_in.at[way, k],
            send_sem=gs.at[way, k], recv_sem=gr.at[way, k],
            device_id=(d, i, to), device_id_type=MESH,
        )

    def advance(way, k, place, to):
        q = lax.rem(i // 2 + k // tiles, pairs)
        t = lax.rem(k, tiles)
        start = pl.multiple_of((1 - way) * half + t * TILE, TILE)
        acc[...] = lax.dot_general(
            xall[q], emb[pl.ds(start, TILE), :], NT, preferred_element_type=jnp.float32
        )

        @pl.when(place > 0)
        def _():
            gauge(way, k, to).wait_recv()
            hop(way, k, to).wait_recv()
            acc[...] += recv_buf[way, k].astype(jnp.float32) * gauge_in[way, k]

        @pl.when(place < nvy - 1)
        def _():
            partial = acc[...]
            span = jnp.maximum(jnp.max(jnp.abs(partial), axis=0, keepdims=True), TINY)
            gauge_out[way, k] = span * (1.0 / TOP)
            send_buf[way, k] = jnp.round(partial * (TOP / span)).astype(jnp.int32).astype(jnp.int16)
            hop(way, k, to).start()
            gauge(way, k, to).start()

        @pl.when(place == nvy - 1)
        def _():
            fin[q, t] = acc[...]

    up, down = j, nvy - 1 - j
    above, below = jnp.minimum(j + 1, nvy - 1), jnp.maximum(j - 1, 0)
    near = jnp.minimum(up, down)

    def step(s, carry):
        k0 = s - LAG * up
        k1 = s - LAG * down
        p = (s - LAG * near) // tiles

        @pl.when((s >= LAG * near) & (s < LAG * near + pieces) & (lax.rem(s - LAG * near, tiles) == 0))
        def _():
            ready(p)

        @pl.when((k0 >= 0) & (k0 < pieces))
        def _():
            advance(0, k0, up, above)

        @pl.when((k1 >= 0) & (k1 < pieces))
        def _():
            advance(1, k1, down, below)

        return carry

    lax.fori_loop(0, pieces + LAG * (nvy - 1), step, 0)

    at_end = (j == 0) | (j == nvy - 1)
    end = jnp.where(j == 0, 0, 1)
    slot = (d * 2 + end) * nvx + i
    owners = pair_rows // rows_dev

    def stat_copy(head, owner_x, owner_y):
        owner = owner_x * nvy + owner_y
        return pltpu.make_async_remote_copy(
            src_ref=st.at[owner], dst_ref=rx.at[slot],
            send_sem=ss.at[head * nvx * nvy + owner], recv_sem=rs.at[slot],
            device_id=(head, owner_x, owner_y), device_id_type=MESH,
        )

    @pl.when(at_end)
    def _():
        base = (i * 2 + jnp.where(j == 0, 0, 1)) * half
        tok = tok_ref[...].astype(jnp.float32)
        for q in range(pairs):
            logits = fin[q]
            peak = jnp.max(jnp.max(logits, axis=0), axis=1, keepdims=True)
            total = jnp.sum(jnp.sum(jnp.exp(logits - peak[None]), axis=0), axis=1, keepdims=True)
            at = lax.broadcasted_iota(jnp.int32, (pair_rows, tok.shape[1]), 1)
            row = lax.broadcasted_iota(jnp.int32, (pair_rows, tok.shape[1]), 0)
            wanted = jnp.sum(
                jnp.where(at == row + (q * pair_rows + d + 1), tok, 0.0), axis=1, keepdims=True
            )
            column = lax.broadcasted_iota(jnp.int32, (pair_rows, TILE), 1)
            hit = jnp.zeros((pair_rows, TILE), jnp.float32)
            for t in range(tiles):
                here = (column + (base + t * TILE)).astype(jnp.float32)
                hit = hit + jnp.where(here == wanted, logits[t], 0.0)
            picked = jnp.sum(hit, axis=1, keepdims=True)
            lane = lax.broadcasted_iota(jnp.int32, (pair_rows, LANES), 1)
            sub = lax.rem(lax.broadcasted_iota(jnp.int32, (pair_rows, LANES), 0), rows_dev)
            packed = jnp.where(lane == sub, peak, 0.0)
            packed = packed + jnp.where(lane == sub + rows_dev, total, 0.0)
            packed = packed + jnp.where(lane == sub + 2 * rows_dev, picked, 0.0)
            packed = jnp.sum(packed.reshape(owners, rows_dev, LANES), axis=1)
            for o in range(owners):
                st[q * owners + o] = packed[o:o + 1]
        rx[slot] = st[i * nvy + j]
        for y in range(nvy):
            for x in reversed(range(nvx)):
                for head in reversed(range(heads)):
                    if head or x or y < nvy - 1:
                        stat_copy(
                            lax.rem(d + head, heads), lax.rem(i + x, nvx), jnp.where(j == 0, nvy - 1 - y, y)
                        ).start()

    for s in range(heads * 2 * nvx):
        head, rest = divmod(s, 2 * nvx)
        side, x = divmod(rest, nvx)
        y = side * (nvy - 1)

        @pl.when((head != d) | (x != i) | (y != j))
        def _(s=s, head=head, x=x, y=y):
            pltpu.make_async_remote_copy(
                src_ref=st.at[0], dst_ref=rx.at[s], send_sem=ss.at[0], recv_sem=rs.at[s],
                device_id=(head, x, y), device_id_type=MESH,
            ).wait_recv()

    result = jnp.zeros((1, LANES), jnp.float32)
    for head in range(heads):
        block = rx[pl.ds(head * 2 * nvx, 2 * nvx)]
        sums = pltpu.roll(block, LANES - rows_dev, 2)
        picks = pltpu.roll(block, LANES - 2 * rows_dev, 2)
        peak = jnp.max(block, axis=0)
        total = jnp.sum(sums * jnp.exp(block - peak[None]), axis=0)
        result = result + (peak + jnp.log(total) - jnp.sum(picks, axis=0))
    out_ref[...] = result[:, :rows_dev]

    for k in range(1, nvy):
        column_copy(lax.rem(j + k, nvy), j).wait_send()
    for k in range(1, nvx):
        to = lax.rem(i + k, nvx)
        for src in range(nvy):
            slice_copy(i, src, to, to).wait_send()

    def drain(k, carry):
        @pl.when(up < nvy - 1)
        def _():
            hop(0, k, above).wait_send()
            gauge(0, k, above).wait_send()

        @pl.when(down < nvy - 1)
        def _():
            hop(1, k, below).wait_send()
            gauge(1, k, below).wait_send()

        return carry

    lax.fori_loop(0, pieces, drain, 0)

    @pl.when(at_end)
    def _():
        for y in range(nvy):
            for x in range(nvx):
                for head in range(heads):
                    if head or x or y < nvy - 1:
                        stat_copy(
                            lax.rem(d + head, heads), lax.rem(i + x, nvx), jnp.where(j == 0, nvy - 1 - y, y)
                        ).wait_send()


def body(sizes, token_ids, hidden, gain, embedding):
    heads, nvx, nvy = sizes
    rows_dev, width = hidden.shape[1:]
    cols = width // nvy
    pairs = nvx // 2
    pair_rows = 2 * nvy * rows_dev
    tiles = embedding.shape[0] // 2 // TILE
    pieces = pairs * tiles
    dma = pltpu.SemaphoreType.DMA
    vmem = pl.BlockSpec(memory_space=pltpu.VMEM)
    out = pl.pallas_call(
        functools.partial(kernel, sizes),
        out_shape=jax.ShapeDtypeStruct((1, rows_dev), jnp.float32),
        in_specs=[vmem, vmem, vmem, pl.BlockSpec(memory_space=pl.ANY)],
        out_specs=vmem,
        scratch_shapes=[
            pltpu.VMEM(embedding.shape, embedding.dtype),
            pltpu.VMEM((nvy, rows_dev, cols), jnp.bfloat16),
            pltpu.VMEM((nvx, nvy, rows_dev, cols), jnp.bfloat16),
            pltpu.VMEM((pairs, pair_rows, cols), jnp.bfloat16),
            pltpu.VMEM((pair_rows, TILE), jnp.float32),
            pltpu.VMEM((2, pieces, pair_rows, TILE), jnp.int16),
            pltpu.VMEM((2, pieces, pair_rows, TILE), jnp.int16),
            pltpu.VMEM((pairs, tiles, pair_rows, TILE), jnp.float32),
            pltpu.VMEM((nvx * nvy, 1, LANES), jnp.float32),
            pltpu.VMEM((heads * 2 * nvx, 1, LANES), jnp.float32),
            pltpu.VMEM((2, pieces, 1, TILE), jnp.float32),
            pltpu.VMEM((2, pieces, 1, TILE), jnp.float32),
            dma((4,)),
            dma((nvy,)),
            dma((nvy,)),
            dma((nvx, nvy)),
            dma((nvx, nvy)),
            dma((2, pieces)),
            dma((2, pieces)),
            dma((2, pieces)),
            dma((2, pieces)),
            dma((heads * nvx * nvy,)),
            dma((heads * 2 * nvx,)),
        ],
        compiler_params=pltpu.CompilerParams(
            collective_id=0, has_side_effects=True, vmem_limit_bytes=62 * 1024 * 1024
        ),
    )(token_ids.reshape(1, -1), hidden, gain, embedding)
    return out.reshape(rows_dev)


def solution(mesh):
    sizes = (mesh.shape["depth"], mesh.shape["vx"], mesh.shape["vy"])
    in_specs = (P(), P("depth", ("vx", "vy"), None), P("depth", None), P("vx", "vy"))
    out_specs = P(("vx", "vy"))
    return jax.shard_map(
        functools.partial(body, sizes), mesh=mesh, in_specs=in_specs, out_specs=out_specs, check_vma=False
    )
```
